32 devices in a mesh: dp: 4 (over y, x), mp: 8 (over z, core).
Axes of the slice: x: 2, y: 2, z: 4, core: 2. Of those that a mesh axis runs over, the one named last changes fastest.
Arguments:
- hidden_in: bfloat16 [256, 8192], P(('dp', 'mp')), may hold values from -6 to 6
- out_grad: bfloat16 [256, 8192], P(('dp', 'mp')), may hold values from -6 to 6
- gate_pre: bfloat16 [256, 28672], P('dp', 'mp'), may hold values from -8 to 8
- up_pre: bfloat16 [256, 28672], P('dp', 'mp'), may hold values from -6 to 6
- down_weight: bfloat16 [28672, 8192], P('mp', 'dp'), may hold values from -0.03125 to 0.03125
- proj_in: bfloat16 [64, 8192], replicated, may hold values from -0.0625 to 0.0625
- proj_grad: bfloat16 [64, 8192], replicated, may hold values from -0.0625 to 0.0625
- proj_hidden: bfloat16 [64, 28672], P(None, 'mp'), may hold values from -0.03125 to 0.03125
- proj_gate: bfloat16 [64, 28672], P(None, 'mp'), may hold values from -0.0625 to 0.0625
- proj_up: bfloat16 [64, 28672], P(None, 'mp'), may hold values from -0.0625 to 0.0625
- doc_lengths: int32 [4, 8], P('dp'), may hold values from 1 to 32, 64 in all within a row
Outputs:
- gate_grad: bfloat16 [256, 28672], P('dp', 'mp')
- up_grad: bfloat16 [256, 28672], P('dp', 'mp')
- sketches: float32 [4, 1536, 64], P('dp', 'mp')
The draws below stay inside these ranges and needn't reach their ends.
Inputs may be any that keep to these rules, and one draw needn't show every extreme that they name: `doc_lengths`: each row holds 8 document lengths, each 1 or more, summing to 64; in every row the largest is exactly 32.
All inputs are finite; a program needn't handle non-finite values.
Results may differ from the reference program's by a relative error of at most 0.0028.
Values may be sent and summed in bfloat16 or wider, within the bound.
A program may use at most 128 MiB of HBM per device.

```python
import math
import jax
import jax.numpy as jnp
import numpy as np
from jax import lax

D = 8192
FF = 28672
RANK = 64
DOCS = 8
PACK_LEN = 64
TOKENS = 256
N_DP = 4


def levels(own_key, extent, cuts, least, largest):
    loudness = 1.0
    for axis_at, shards_of in cuts:
        heights = jax.random.uniform(jax.random.fold_in(jax.random.fold_in(own_key, 6), axis_at), (shards_of,), jnp.float32, least / len(cuts), largest / len(cuts))
        loudness = loudness * jnp.repeat(jnp.exp(heights), extent[axis_at] // shards_of).reshape((-1,) + (1,) * (len(extent) - 1 - axis_at))
    return loudness


def split_up(amount, total, most, slope):
    loads = [(1 << 20) // math.isqrt(standing ** slope) + 1 for standing in range(2, amount + 1)]
    rest, given = total - most - (amount - 1), [1] * (amount - 1)
    while rest > 0:
        movable = [i for i in range(amount - 1) if given[i] < most]
        pool, remaining = sum([loads[i] for i in movable]), rest
        for i in movable:
            extra = min(most - given[i], max(1, remaining * loads[i] // pool), rest)
            given[i] = given[i] + extra
            rest = rest - extra
    return np.array([most] + given)


def ragged(rng, count, total, bound, skew):
    if count == 2:
        one = jax.random.randint(rng, (), max(1, total - bound), min(bound, total - 1) + 1)
        return jnp.stack([one, total - one])
    tallies = jnp.asarray(split_up(count, total, bound, skew), jnp.int32)
    pairs = (count - 1) // 2
    donor, receiver = tallies[1:1 + 2 * pairs:2], tallies[2:2 + 2 * pairs:2]
    room = jnp.minimum(donor - 1, bound - receiver)
    passed = jax.random.randint(jax.random.fold_in(rng, 1), (pairs,), 0, 1 << 20) % (room + 1)
    tallies = tallies.at[1:1 + 2 * pairs:2].set(donor - passed).at[2:2 + 2 * pairs:2].set(receiver + passed)
    return tallies[jax.random.permutation(jax.random.fold_in(rng, 2), count)]


def noise(stream_key, shape, scale, reach, cuts=(), kind=jnp.bfloat16):
    entries = jax.random.normal(stream_key, shape, jnp.float32) * scale
    if len(cuts) > 0:
        entries = levels(stream_key, shape, cuts, -0.22, 0.18) * entries
    return jnp.clip(entries, min=-reach, max=reach).astype(kind)


def setup_inputs(seed: int = 0) -> dict:
    splits = jax.random.split(jax.random.key(seed), 12)
    return {
        "hidden_in": noise(splits[0], (TOKENS, D), 1.0, 6.0, ((0, 32),)),
        "out_grad": noise(splits[1], (TOKENS, D), 1.0, 6.0, ((0, 32),)),
        "gate_pre": noise(splits[2], (TOKENS, FF), 1.5, 8.0, ((0, 4), (1, 8))),
        "up_pre": noise(splits[3], (TOKENS, FF), 1.0, 6.0, ((0, 4), (1, 8))),
        "down_weight": noise(splits[4], (FF, D), FF ** -0.5, 0.03125, ((0, 8), (1, 4))),
        "proj_in": noise(splits[5], (RANK, D), D ** -0.5, 0.0625),
        "proj_grad": noise(splits[6], (RANK, D), D ** -0.5, 0.0625),
        "proj_hidden": noise(splits[7], (RANK, FF), FF ** -0.5, 0.03125, ((1, 8),)),
        "proj_gate": noise(splits[8], (RANK, FF), (FF // 4) ** -0.5, 0.0625, ((1, 8),)),
        "proj_up": noise(splits[9], (RANK, FF), (FF // 4) ** -0.5, 0.0625, ((1, 8),)),
        "doc_lengths": jax.vmap(lambda own: ragged(own, DOCS, PACK_LEN, PACK_LEN // 2, 2))(jax.random.split(splits[10], N_DP)).reshape((N_DP, DOCS)).astype(jnp.int32),
    }


def sketch_of(member, first_side, second_side):
    masked = (member[:, :, None] * first_side[:, None, :]).reshape(first_side.shape[0], -1)
    return jnp.dot(masked.T, second_side, precision=lax.Precision.HIGHEST)


def reference(hidden_in, out_grad, gate_pre, up_pre, down_weight, proj_in, proj_grad, proj_hidden, proj_gate, proj_up, doc_lengths):
    def one_pack(items):
        inputs, grads, gates, ups, doc_sizes = items
        gate_value = gates.astype(jnp.float32)
        up_value = ups.astype(jnp.float32)
        sigmoid_gate = jax.nn.sigmoid(gate_value)
        silu_gate = gate_value * sigmoid_gate
        hidden = (silu_gate * up_value).astype(jnp.bfloat16)
        grad_hidden = jnp.dot(grads, down_weight.T, preferred_element_type=jnp.float32)
        gate_grad = (grad_hidden * up_value * sigmoid_gate * (1.0 + gate_value * (1.0 - sigmoid_gate))).astype(jnp.bfloat16)
        up_grad = (grad_hidden * silu_gate).astype(jnp.bfloat16)
        hidden_side = jnp.dot(hidden, proj_hidden.T, preferred_element_type=jnp.float32)
        gate_side = jnp.dot(gate_grad, proj_gate.T, preferred_element_type=jnp.float32)
        up_side = jnp.dot(up_grad, proj_up.T, preferred_element_type=jnp.float32)
        grad_side = jnp.dot(grads, proj_grad.T, preferred_element_type=jnp.float32)
        input_side = jnp.dot(inputs, proj_in.T, preferred_element_type=jnp.float32)
        starts = jnp.cumsum(doc_sizes) - doc_sizes
        positions = jnp.arange(PACK_LEN, dtype=jnp.int32)[:, None]
        member = ((positions >= starts[None, :]) & (positions < (starts + doc_sizes)[None, :])).astype(jnp.float32)
        sketch_all = jnp.concatenate([sketch_of(member, hidden_side, grad_side), sketch_of(member, input_side, gate_side), sketch_of(member, input_side, up_side)], axis=0)
        return gate_grad, up_grad, sketch_all

    gate_grad, up_grad, sketches = lax.map(one_pack, (hidden_in.reshape(N_DP, PACK_LEN, D), out_grad.reshape(N_DP, PACK_LEN, D), gate_pre.reshape(N_DP, PACK_LEN, FF), up_pre.reshape(N_DP, PACK_LEN, FF), doc_lengths))
    return gate_grad.reshape(TOKENS, FF), up_grad.reshape(TOKENS, FF), sketches
```

```python
import jax
import jax.numpy as jnp
from jax import lax
from jax.sharding import PartitionSpec as P


def own_sketch_rows(sides, doc_sizes, rank, row_count):
    hidden, gate, up, grad, inp = [sides[:, s * rank : (s + 1) * rank] for s in range(5)]
    firsts = jnp.concatenate([hidden, inp, inp], axis=1)
    seconds = jnp.concatenate([grad, gate, up], axis=1)
    docs = doc_sizes.shape[0]
    r = lax.axis_index("mp") * row_count + jnp.arange(row_count, dtype=jnp.int32)
    which, doc, lane = r // (docs * rank), (r // rank) % docs, r % rank
    pick = (jnp.arange(3 * rank)[:, None] == (which * rank + lane)[None, :]).astype(jnp.float32)
    chosen = jnp.dot(firsts, pick, precision=lax.Precision.HIGHEST)
    ends = jnp.cumsum(doc_sizes)
    of_doc = doc[None, :] == jnp.arange(docs)[:, None]
    end = jnp.sum(jnp.where(of_doc, ends[:, None], 0), axis=0)
    start = jnp.sum(jnp.where(of_doc, (ends - doc_sizes)[:, None], 0), axis=0)
    t = jnp.arange(sides.shape[0], dtype=jnp.int32)[:, None]
    masked = jnp.where((t >= start[None, :]) & (t < end[None, :]), chosen, 0.0)
    full = jnp.dot(masked.T, seconds, precision=lax.Precision.HIGHEST)
    out = jnp.zeros((row_count, rank), jnp.float32)
    for w in range(3):
        out = out + jnp.where((which == w)[:, None], full[:, w * rank : (w + 1) * rank], 0.0)
    return out


def local(
    hidden_in,
    out_grad,
    gate_pre,
    up_pre,
    down_weight,
    proj_in,
    proj_grad,
    proj_hidden,
    proj_gate,
    proj_up,
    doc_lengths,
):
    n_dp, n_mp = lax.axis_size("dp"), lax.axis_size("mp")
    own_rows, rank = hidden_in.shape[0], proj_in.shape[0]
    pack, units = gate_pre.shape
    me = lax.axis_index("dp")
    turned = lax.all_to_all(out_grad, "dp", split_axis=1, concat_axis=0, tiled=True)
    gathered = lax.all_gather(turned.reshape(n_dp, own_rows, -1), "mp", axis=1)
    gathered = gathered.reshape(n_dp * pack, -1)
    partial = lax.dot_general(
        gathered, down_weight, (((1,), (1,)), ((), ())), preferred_element_type=jnp.float32
    ).reshape(n_dp, pack, units)
    arrived = lax.all_to_all(
        partial.astype(jnp.bfloat16), "dp", split_axis=0, concat_axis=0, tiled=True
    )
    own = lax.dynamic_index_in_dim(partial, me, 0, keepdims=False)
    others = jnp.where(
        (jnp.arange(n_dp) == me)[:, None, None], 0.0, arrived.astype(jnp.float32)
    )
    grad_hidden = own + jnp.sum(others, axis=0)
    gate_value = gate_pre.astype(jnp.float32)
    up_value = up_pre.astype(jnp.float32)
    sigmoid_gate = jax.nn.sigmoid(gate_value)
    silu_gate = gate_value * sigmoid_gate
    hidden = (silu_gate * up_value).astype(jnp.bfloat16)
    gate_grad = (
        grad_hidden * up_value * sigmoid_gate * (1.0 + gate_value * (1.0 - sigmoid_gate))
    ).astype(jnp.bfloat16)
    up_grad = (grad_hidden * silu_gate).astype(jnp.bfloat16)
    hidden_side = jnp.dot(hidden, proj_hidden.T, preferred_element_type=jnp.float32)
    gate_side = jnp.dot(gate_grad, proj_gate.T, preferred_element_type=jnp.float32)
    up_side = jnp.dot(up_grad, proj_up.T, preferred_element_type=jnp.float32)
    grad_side = jnp.dot(out_grad, proj_grad.T, preferred_element_type=jnp.float32)
    input_side = jnp.dot(hidden_in, proj_in.T, preferred_element_type=jnp.float32)
    stacked = jnp.concatenate([hidden_side, gate_side, up_side], axis=1)
    own_sides = lax.psum_scatter(stacked, "mp", scatter_dimension=0, tiled=True)
    sides = lax.all_gather(
        jnp.concatenate([own_sides, grad_side, input_side], axis=1), "mp", axis=0, tiled=True
    )
    docs = doc_lengths.shape[1]
    sketches = own_sketch_rows(sides, doc_lengths[0], rank, 3 * docs * rank // n_mp)
    return (gate_grad, up_grad, sketches[None])


def solution(mesh):
    placed = (
        P(("dp", "mp"), None),
        P(("dp", "mp"), None),
        P("dp", "mp"),
        P("dp", "mp"),
        P("mp", "dp"),
        P(),
        P(),
        P(None, "mp"),
        P(None, "mp"),
        P(None, "mp"),
        P("dp", None),
    )
    return jax.shard_map(
        local,
        mesh=mesh,
        in_specs=placed,
        out_specs=(P("dp", "mp"), P("dp", "mp"), P("dp", "mp", None)),
        check_vma=False,
    )
```

```python
import functools

import jax
import jax.numpy as jnp
from jax import lax
from jax.experimental import pallas as pl
from jax.experimental.pallas import tpu as pltpu
from jax.sharding import PartitionSpec as P

LANES = 128
F32 = jnp.float32
BF16 = jnp.bfloat16
NT = (((1,), (1,)), ((), ()))


def round_up(value, step):
    return -(-value // step) * step


def dot_nt(a, b):
    return lax.dot_general(a, b, NT, preferred_element_type=F32)


def kernel(
    n_dp,
    n_mp,
    chunk,
    hidden_in,
    out_grad,
    doc_sizes,
    gate_hbm,
    up_hbm,
    weight_hbm,
    proj_in_hbm,
    proj_grad_hbm,
    proj_hidden_hbm,
    proj_gate_hbm,
    proj_up_hbm,
    gate_grad,
    up_grad,
    sketches,
    gate_pre,
    up_pre,
    weight,
    proj_in,
    proj_grad,
    proj_hidden,
    proj_gate,
    proj_up,
    stage,
    lhs,
    own_part,
    send_part,
    recv_part,
    gate_factor,
    up_factor,
    stack,
    stack_in,
    sides,
    load_sem,
    weight_sem,
    own_sem,
    turn_send,
    turn_recv,
    row_send,
    row_recv,
    pair_send,
    pair_recv,
    part_send,
    part_recv,
    scatter_send,
    scatter_recv,
    gather_send,
    gather_recv,
):
    dp, mp = lax.axis_index("dp"), lax.axis_index("mp")
    pack, units = gate_pre.shape
    own_rows, features = out_grad.shape[0], weight.shape[1]
    rank = proj_in.shape[0]
    n_chunks = units // chunk
    n_row = n_mp // 2
    row, core = mp // 2, mp % 2
    mesh_id = pl.DeviceIdType.MESH

    def remote(src, dst, send, recv, device):
        return pltpu.make_async_remote_copy(
            src_ref=src, dst_ref=dst, send_sem=send, recv_sem=recv,
            device_id=device, device_id_type=mesh_id,
        )

    def dp_peer(k):
        return lax.rem(dp + k, n_dp)

    def dp_source(k):
        return lax.rem(dp + n_dp - k, n_dp)

    barrier = pltpu.get_barrier_semaphore()
    for k in range(1, n_dp):
        pl.semaphore_signal(barrier, inc=1, device_id=(dp_peer(k), mp), device_id_type=mesh_id)
    for k in range(1, n_mp):
        pl.semaphore_signal(
            barrier, inc=1, device_id=(dp, lax.rem(mp + k, n_mp)), device_id_type=mesh_id
        )

    own_columns = pl.ds(pl.multiple_of(dp * features, LANES), features)
    own_copy = pltpu.make_async_copy(out_grad.at[:, own_columns], stage.at[mp, dp], own_sem)
    own_copy.start()
    loads = [
        pltpu.make_async_copy(src, dst, load_sem.at[n])
        for n, (src, dst) in enumerate(
            [
                (gate_hbm, gate_pre),
                (up_hbm, up_pre),
                (proj_hidden_hbm, proj_hidden),
                (proj_grad_hbm, proj_grad),
                (proj_in_hbm, proj_in),
                (proj_gate_hbm, proj_gate),
                (proj_up_hbm, proj_up),
            ]
        )
    ]
    for load in loads:
        load.start()

    def weight_load(j):
        rows = pl.ds(pl.multiple_of(j * chunk, 16), chunk)
        return pltpu.make_async_copy(weight_hbm.at[rows], weight.at[rows], weight_sem.at[j])

    for j in range(n_chunks):
        weight_load(j).start()

    pl.semaphore_wait(barrier, n_dp - 1 + n_mp - 1)

    turns = []
    for k in range(1, n_dp):
        peer = dp_peer(k)
        columns = pl.ds(pl.multiple_of(peer * features, LANES), features)
        turn = remote(
            out_grad.at[:, columns], stage.at[mp, dp], turn_send.at[k - 1], turn_recv.at[k - 1],
            (peer, mp),
        )
        turn.start()
        turns.append(turn)
    own_copy.wait()
    for k in range(1, n_dp):
        landing = stage.at[mp, dp_source(k)]
        remote(landing, landing, turn_send.at[k - 1], turn_recv.at[k - 1], (dp, mp)).wait_recv()

    partner = (dp, row * 2 + (1 - core))
    sends = list(turns)
    mine = stage.at[mp]
    for k in range(1, n_row):
        copy = remote(
            mine, mine, row_send.at[k - 1], row_recv.at[k - 1],
            (dp, lax.rem(row + k, n_row) * 2 + core),
        )
        copy.start()
        sends.append(copy)
    copy = remote(mine, mine, pair_send.at[0], pair_recv.at[0], partner)
    copy.start()
    sends.append(copy)

    loads[0].wait()
    loads[1].wait()
    loads[2].wait()
    hidden_side = jnp.zeros((pack, rank), F32)
    for j in range(n_chunks):
        at = slice(j * chunk, (j + 1) * chunk)
        gate_value = gate_pre[:, at].astype(F32)
        up_value = up_pre[:, at].astype(F32)
        sigmoid_gate = 1.0 / (1.0 + jnp.exp(-gate_value))
        silu_gate = gate_value * sigmoid_gate
        hidden = (silu_gate * up_value).astype(BF16)
        gate_factor[j] = up_value * sigmoid_gate * (1.0 + gate_value * (1.0 - sigmoid_gate))
        up_factor[j] = silu_gate
        hidden_side = hidden_side + dot_nt(hidden, proj_hidden[:, at])
    stack[...] = jnp.zeros(stack.shape, F32)
    stack[:, :, 0:rank] = hidden_side.reshape(n_mp, own_rows, rank)
    loads[3].wait()
    grad_side = dot_nt(out_grad[...], proj_grad[...])
    loads[4].wait()
    input_side = dot_nt(hidden_in[...], proj_in[...])
    loads[5].wait()
    loads[6].wait()

    def assemble(source_row):
        for k in range(n_dp):
            owner = dp_peer(k)
            both = [stage[source_row * 2 + c, owner].astype(F32) for c in range(2)]
            at = pl.ds(pl.multiple_of(k * pack + source_row * 2 * own_rows, 16), 2 * own_rows)
            lhs[at, :] = jnp.concatenate(both, axis=0).astype(BF16)

    for k in range(1, n_row):
        source = lax.rem(row + n_row - k, n_row)
        landing = stage.at[source * 2 + core]
        remote(landing, landing, row_send.at[k - 1], row_recv.at[k - 1], (dp, mp)).wait_recv()
        copy = remote(landing, landing, pair_send.at[k], pair_recv.at[k], partner)
        copy.start()
        sends.append(copy)
    for k in range(n_row):
        source = lax.rem(row + n_row - k, n_row)
        landing = stage.at[source * 2 + (1 - core)]
        remote(landing, landing, pair_send.at[k], pair_recv.at[k], partner).wait_recv()
        assemble(source)

    def part_copy(j, k):
        return remote(
            send_part.at[j, k - 1], recv_part.at[j, k - 1], part_send.at[j, k - 1],
            part_recv.at[j, k - 1], (dp_peer(k), mp),
        )

    def multiply(j, carry):
        weight_load(j).wait()
        rows = pl.ds(pl.multiple_of(j * chunk, 16), chunk)
        part = dot_nt(lhs[...], weight[rows, :])
        for k in range(1, n_dp):
            send_part[j, k - 1] = part[k * pack : (k + 1) * pack].astype(BF16)
            part_copy(j, k).start()
        own_part[j] = part[:pack]
        return carry

    lax.fori_loop(0, n_chunks, multiply, 0)

    gate_side = jnp.zeros((pack, rank), F32)
    up_side = jnp.zeros((pack, rank), F32)
    for j in range(n_chunks):
        at = slice(j * chunk, (j + 1) * chunk)
        total = own_part[j]
        for k in range(1, n_dp):
            part_copy(j, k).wait_recv()
            total = total + recv_part[j, k - 1].astype(F32)
        gate_new = (total * gate_factor[j]).astype(BF16)
        up_new = (total * up_factor[j]).astype(BF16)
        gate_grad[:, at] = gate_new
        up_grad[:, at] = up_new
        gate_side = gate_side + dot_nt(gate_new, proj_gate[:, at])
        up_side = up_side + dot_nt(up_new, proj_up[:, at])
    stack[:, :, rank : 2 * rank] = gate_side.reshape(n_mp, own_rows, rank)
    stack[:, :, 2 * rank : 3 * rank] = up_side.reshape(n_mp, own_rows, rank)

    for k in range(1, n_mp):
        peer = lax.rem(mp + k, n_mp)
        copy = remote(
            stack.at[peer], stack_in.at[k - 1], scatter_send.at[k - 1], scatter_recv.at[k - 1],
            (dp, peer),
        )
        copy.start()
        sends.append(copy)
    own_sum = stack[mp]
    for k in range(1, n_mp):
        landing = stack_in.at[k - 1]
        remote(
            landing, landing, scatter_send.at[k - 1], scatter_recv.at[k - 1], (dp, mp)
        ).wait_recv()
        own_sum = own_sum + stack_in[k - 1]
    width = stack.shape[2]
    sides[mp] = jnp.zeros(sides.shape[1:], F32)
    sides[mp, :, :width] = own_sum
    sides[mp, :, 3 * rank : 4 * rank] = grad_side
    sides[mp, :, 4 * rank : 5 * rank] = input_side
    for k in range(1, n_mp):
        peer = lax.rem(mp + k, n_mp)
        copy = remote(
            sides.at[mp], sides.at[mp], gather_send.at[k - 1], gather_recv.at[k - 1], (dp, peer)
        )
        copy.start()
        sends.append(copy)

    row_count, docs = sketches.shape[1], doc_sizes.shape[1]
    rank_bits, doc_bits = rank.bit_length() - 1, docs.bit_length() - 1
    wide = sides.shape[2]

    def row_ids(columns):
        return mp * row_count + lax.broadcasted_iota(jnp.int32, (row_count, columns), 0)

    def which_of(ids):
        return lax.shift_right_logical(ids, rank_bits + doc_bits)

    ids = row_ids(wide)
    column = lax.broadcasted_iota(jnp.int32, ids.shape, 1)
    base = jnp.where(which_of(ids) == 0, 0, 4 * rank)
    pick = (column == base + (ids & (rank - 1))).astype(F32)
    ids = row_ids(pack)
    doc = lax.shift_right_logical(ids, rank_bits) & (docs - 1)
    start = jnp.zeros(ids.shape, jnp.int32)
    end = jnp.zeros(ids.shape, jnp.int32)
    passed = jnp.int32(0)
    for k in range(docs):
        after = passed + doc_sizes[0, k]
        start = jnp.where(doc == k, passed, start)
        end = jnp.where(doc == k, after, end)
        passed = after
    token = lax.broadcasted_iota(jnp.int32, ids.shape, 1)
    member = (token >= start) & (token < end)

    for k in range(1, n_mp):
        landing = sides.at[lax.rem(mp + n_mp - k, n_mp)]
        remote(
            landing, landing, gather_send.at[k - 1], gather_recv.at[k - 1], (dp, mp)
        ).wait_recv()
    full = sides[...].reshape(pack, wide)
    chosen = lax.dot_general(
        pick, full, NT, precision=lax.Precision.HIGHEST, preferred_element_type=F32
    )
    masked = jnp.where(member, chosen, 0.0)
    product = jnp.dot(
        masked, full, precision=lax.Precision.HIGHEST, preferred_element_type=F32
    )
    which = which_of(row_ids(rank))
    sketches[0] = jnp.where(
        which == 0,
        product[:, 3 * rank : 4 * rank],
        jnp.where(which == 1, product[:, rank : 2 * rank], product[:, 2 * rank : 3 * rank]),
    )

    for copy in sends:
        copy.wait_send()
    for j in range(n_chunks):
        for k in range(1, n_dp):
            part_copy(j, k).wait_send()


def local(
    hidden_in,
    out_grad,
    gate_pre,
    up_pre,
    down_weight,
    proj_in,
    proj_grad,
    proj_hidden,
    proj_gate,
    proj_up,
    doc_lengths,
):
    n_dp, n_mp = lax.axis_size("dp"), lax.axis_size("mp")
    own_rows, rank = hidden_in.shape[0], proj_in.shape[0]
    pack, units = gate_pre.shape
    features = down_weight.shape[1]
    docs = doc_lengths.shape[1]
    chunk = 4 * LANES
    if units % chunk:
        chunk = units
    n_chunks = units // chunk
    width, wide = round_up(3 * rank, LANES), round_up(5 * rank, LANES)
    dma = pltpu.SemaphoreType.DMA
    vmem = pl.BlockSpec(memory_space=pltpu.VMEM)
    far = pl.BlockSpec(memory_space=pl.ANY)
    return pl.pallas_call(
        functools.partial(kernel, n_dp, n_mp, chunk),
        out_shape=(
            jax.ShapeDtypeStruct((pack, units), BF16),
            jax.ShapeDtypeStruct((pack, units), BF16),
            jax.ShapeDtypeStruct((1, 3 * docs * rank // n_mp, rank), F32),
        ),
        in_specs=[vmem, vmem, pl.BlockSpec(memory_space=pltpu.SMEM)] + [far] * 8,
        out_specs=(vmem, vmem, vmem),
        scratch_shapes=[
            pltpu.VMEM((pack, units), BF16),
            pltpu.VMEM((pack, units), BF16),
            pltpu.VMEM((units, features), BF16),
            pltpu.VMEM(proj_in.shape, BF16),
            pltpu.VMEM(proj_grad.shape, BF16),
            pltpu.VMEM((rank, units), BF16),
            pltpu.VMEM((rank, units), BF16),
            pltpu.VMEM((rank, units), BF16),
            pltpu.VMEM((n_mp, n_dp, own_rows, features), BF16),
            pltpu.VMEM((n_dp * pack, features), BF16),
            pltpu.VMEM((n_chunks, pack, chunk), F32),
            pltpu.VMEM((n_chunks, n_dp - 1, pack, chunk), BF16),
            pltpu.VMEM((n_chunks, n_dp - 1, pack, chunk), BF16),
            pltpu.VMEM((n_chunks, pack, chunk), F32),
            pltpu.VMEM((n_chunks, pack, chunk), F32),
            pltpu.VMEM((n_mp, own_rows, width), F32),
            pltpu.VMEM((n_mp - 1, own_rows, width), F32),
            pltpu.VMEM((n_mp, own_rows, wide), F32),
            dma((7,)),
            dma((n_chunks,)),
            dma,
            dma((n_dp - 1,)),
            dma((n_dp - 1,)),
            dma((n_mp // 2 - 1,)),
            dma((n_mp // 2 - 1,)),
            dma((n_mp // 2,)),
            dma((n_mp // 2,)),
            dma((n_chunks, n_dp - 1)),
            dma((n_chunks, n_dp - 1)),
            dma((n_mp - 1,)),
            dma((n_mp - 1,)),
            dma((n_mp - 1,)),
            dma((n_mp - 1,)),
        ],
        compiler_params=pltpu.CompilerParams(
            collective_id=0, has_side_effects=True, vmem_limit_bytes=60 * 1024 * 1024
        ),
    )(
        hidden_in,
        out_grad,
        doc_lengths,
        gate_pre,
        up_pre,
        down_weight,
        proj_in,
        proj_grad,
        proj_hidden,
        proj_gate,
        proj_up,
    )


def solution(mesh):
    placed = (
        P(("dp", "mp"), None),
        P(("dp", "mp"), None),
        P("dp", "mp"),
        P("dp", "mp"),
        P("mp", "dp"),
        P(),
        P(),
        P(None, "mp"),
        P(None, "mp"),
        P(None, "mp"),
        P("dp", None),
    )
    return jax.shard_map(
        local,
        mesh=mesh,
        in_specs=placed,
        out_specs=(P("dp", "mp"), P("dp", "mp"), P("dp", "mp", None)),
        check_vma=False,
    )
```

```python
import functools

import jax
import jax.numpy as jnp
from jax import lax
from jax.experimental import pallas as pl
from jax.experimental.pallas import tpu as pltpu
from jax.sharding import PartitionSpec as P

LANES = 128
F32 = jnp.float32
BF16 = jnp.bfloat16
NT = (((1,), (1,)), ((), ()))


def dot_nt(a, b):
    return lax.dot_general(a, b, NT, preferred_element_type=F32)


def kernel(
    n_dp,
    n_mp,
    chunk,
    hidden_in,
    out_grad,
    doc_sizes,
    gate_hbm,
    up_hbm,
    weight_hbm,
    proj_in_hbm,
    proj_grad_hbm,
    proj_hidden_hbm,
    proj_gate_hbm,
    proj_up_hbm,
    gate_grad,
    up_grad,
    sketches,
    gate_pre,
    up_pre,
    weight,
    proj_in,
    proj_grad,
    proj_hidden,
    proj_gate,
    proj_up,
    stage,
    lhs,
    own_part,
    send_part,
    recv_part,
    gate_factor,
    up_factor,
    side_part,
    side_in,
    side_sum,
    row_sides,
    masked,
    load_sem,
    weight_sem,
    own_sem,
    turn_send,
    turn_recv,
    row_send,
    row_recv,
    pair_send,
    pair_recv,
    part_send,
    part_recv,
    side_send,
    side_recv,
    gather_send,
    gather_recv,
):
    dp, mp = lax.axis_index("dp"), lax.axis_index("mp")
    pack, units = gate_pre.shape
    own_rows, features = out_grad.shape[0], weight.shape[1]
    rank = proj_in.shape[0]
    n_chunks = units // chunk
    n_row = n_mp // 2
    row, core = mp // 2, mp % 2
    half = n_row // 2
    half_pack = pack // 2
    row_count, docs = sketches.shape[1], doc_sizes.shape[1]
    rank_bits, doc_bits = rank.bit_length() - 1, docs.bit_length() - 1
    mesh_id = pl.DeviceIdType.MESH

    def remote(src, dst, send, recv, device):
        return pltpu.make_async_remote_copy(
            src_ref=src, dst_ref=dst, send_sem=send, recv_sem=recv,
            device_id=device, device_id_type=mesh_id,
        )

    def dp_peer(k):
        return lax.rem(dp + k, n_dp)

    def dp_source(k):
        return lax.rem(dp + n_dp - k, n_dp)

    def half_of(g):
        return row // half if g == 0 else 1 - row // half

    def row_peer(k):
        return half_of(k // half) * half + lax.rem(row % half + k % half, half)

    def row_source(k):
        return half_of(k // half) * half + lax.rem(row % half + half - k % half, half)

    def needs(device, w):
        block = docs * rank
        return (device * row_count < (w + 1) * block) & ((device + 1) * row_count > w * block)

    barrier = pltpu.get_barrier_semaphore()
    for k in range(1, n_dp):
        pl.semaphore_signal(barrier, inc=1, device_id=(dp_peer(k), mp), device_id_type=mesh_id)
    for k in range(1, n_mp):
        pl.semaphore_signal(
            barrier, inc=1, device_id=(dp, lax.rem(mp + k, n_mp)), device_id_type=mesh_id
        )

    own_columns = pl.ds(pl.multiple_of(dp * features, LANES), features)
    own_copy = pltpu.make_async_copy(out_grad.at[:, own_columns], stage.at[mp, dp], own_sem)
    own_copy.start()
    loads = [
        pltpu.make_async_copy(src, dst, load_sem.at[n])
        for n, (src, dst) in enumerate(
            [
                (gate_hbm, gate_pre),
                (up_hbm, up_pre),
                (proj_hidden_hbm, proj_hidden),
                (proj_grad_hbm, proj_grad),
                (proj_in_hbm, proj_in),
                (proj_gate_hbm, proj_gate),
                (proj_up_hbm, proj_up),
            ]
        )
    ]
    for load in loads:
        load.start()

    def weight_load(j):
        rows = pl.ds(pl.multiple_of(j * chunk, 16), chunk)
        return pltpu.make_async_copy(weight_hbm.at[rows], weight.at[rows], weight_sem.at[j])

    for j in range(n_chunks):
        weight_load(j).start()

    pl.semaphore_wait(barrier, n_dp - 1 + n_mp - 1)

    turns = []
    for k in range(1, n_dp):
        peer = dp_peer(k)
        columns = pl.ds(pl.multiple_of(peer * features, LANES), features)
        turn = remote(
            out_grad.at[:, columns], stage.at[mp, dp], turn_send.at[k - 1], turn_recv.at[k - 1],
            (peer, mp),
        )
        turn.start()
        turns.append(turn)
    own_copy.wait()
    for k in range(1, n_dp):
        landing = stage.at[mp, dp_source(k)]
        remote(landing, landing, turn_send.at[k - 1], turn_recv.at[k - 1], (dp, mp)).wait_recv()

    partner = (dp, row * 2 + (1 - core))
    sends = list(turns)
    mine = stage.at[mp]
    copy = remote(mine, mine, pair_send.at[0], pair_recv.at[0], partner)
    copy.start()
    sends.append(copy)
    for k in range(1, n_row):
        copy = remote(
            mine, mine, row_send.at[k - 1], row_recv.at[k - 1], (dp, row_peer(k) * 2 + core)
        )
        copy.start()
        sends.append(copy)

    loads[0].wait()
    loads[1].wait()
    loads[2].wait()
    hidden_side = jnp.zeros((pack, rank), F32)
    for j in range(n_chunks):
        at = slice(j * chunk, (j + 1) * chunk)
        gate_value = gate_pre[:, at].astype(F32)
        up_value = up_pre[:, at].astype(F32)
        sigmoid_gate = 1.0 / (1.0 + jnp.exp(-gate_value))
        silu_gate = gate_value * sigmoid_gate
        hidden = (silu_gate * up_value).astype(BF16)
        gate_factor[j] = up_value * sigmoid_gate * (1.0 + gate_value * (1.0 - sigmoid_gate))
        up_factor[j] = silu_gate
        hidden_side = hidden_side + dot_nt(hidden, proj_hidden[:, at])

    def side_copy(w, k):
        peer = lax.rem(mp + k, n_mp)
        return remote(
            side_part.at[w], side_in.at[w, k - 1], side_send.at[w, k - 1],
            side_recv.at[w, k - 1], (dp, peer),
        )

    def send_side(w, value):
        side_part[w, :, :rank] = value[:half_pack]
        side_part[w, :, rank:] = value[half_pack:]
        for k in range(1, n_mp):
            @pl.when(needs(lax.rem(mp + k, n_mp), w))
            def _():
                side_copy(w, k).start()

    def sum_side(w):
        @pl.when(needs(mp, w))
        def _():
            value = side_part[w]
            for k in range(1, n_mp):
                side_copy(w, k).wait_recv()
                value = value + side_in[w, k - 1]
            side_sum[w, :half_pack] = value[:, :rank]
            side_sum[w, half_pack:] = value[:, rank:]

    side_sum[...] = jnp.zeros(side_sum.shape, F32)
    send_side(0, hidden_side)

    def assemble(g, source_row):
        for k in range(n_dp):
            owner = dp_peer(k)
            both = [stage[source_row * 2 + c, owner].astype(F32) for c in range(2)]
            at = pl.ds(
                pl.multiple_of(k * half_pack + (source_row % half) * 2 * own_rows, 16),
                2 * own_rows,
            )
            lhs[g, at, :] = jnp.concatenate(both, axis=0).astype(BF16)

    def part_copy(g, j, k):
        return remote(
            send_part.at[g, j, k - 1], recv_part.at[g, j, k - 1], part_send.at[g, j, k - 1],
            part_recv.at[g, j, k - 1], (dp_peer(k), mp),
        )

    def half_step(g):
        for k in range(g * half, (g + 1) * half):
            if k == 0:
                continue
            landing = stage.at[row_source(k) * 2 + core]
            remote(landing, landing, row_send.at[k - 1], row_recv.at[k - 1], partner).wait_recv()
            copy = remote(landing, landing, pair_send.at[k], pair_recv.at[k], partner)
            copy.start()
            sends.append(copy)
        for k in range(g * half, (g + 1) * half):
            landing = stage.at[row_source(k) * 2 + (1 - core)]
            remote(landing, landing, pair_send.at[k], pair_recv.at[k], partner).wait_recv()
            assemble(g, row_source(k))

        def multiply(j, carry):
            if g == 0:
                weight_load(j).wait()
            rows = pl.ds(pl.multiple_of(j * chunk, 16), chunk)
            part = dot_nt(lhs[g], weight[rows, :])
            for k in range(1, n_dp):
                send_part[g, j, k - 1] = part[k * half_pack : (k + 1) * half_pack].astype(BF16)
                part_copy(g, j, k).start()
            own_part[g, j] = part[:half_pack]
            return carry

        lax.fori_loop(0, n_chunks, multiply, 0)

    half_step(0)
    loads[3].wait()
    row_sides[mp, :, :rank] = dot_nt(out_grad[...], proj_grad[...])
    loads[4].wait()
    row_sides[mp, :, rank:] = dot_nt(hidden_in[...], proj_in[...])
    for k in range(1, n_mp):
        mine = row_sides.at[mp]
        copy = remote(
            mine, mine, gather_send.at[k - 1], gather_recv.at[k - 1], (dp, lax.rem(mp + k, n_mp))
        )
        copy.start()
        sends.append(copy)
    loads[5].wait()
    loads[6].wait()
    half_step(1)

    def row_ids(columns):
        return mp * row_count + lax.broadcasted_iota(jnp.int32, (row_count, columns), 0)

    def which_of(ids):
        return lax.shift_right_logical(ids, rank_bits + doc_bits)

    def precise(a, b, dims):
        return lax.dot_general(
            a, b, dims, precision=lax.Precision.HIGHEST, preferred_element_type=F32
        )

    ids = row_ids(rank)
    which = which_of(ids)
    column = lax.broadcasted_iota(jnp.int32, ids.shape, 1)
    pick = (column == (ids & (rank - 1))).astype(F32)
    ids = row_ids(pack)
    doc = lax.shift_right_logical(ids, rank_bits) & (docs - 1)
    start = jnp.zeros(ids.shape, jnp.int32)
    end = jnp.zeros(ids.shape, jnp.int32)
    passed = jnp.int32(0)
    for k in range(docs):
        after = passed + doc_sizes[0, k]
        start = jnp.where(doc == k, passed, start)
        end = jnp.where(doc == k, after, end)
        passed = after
    token = lax.broadcasted_iota(jnp.int32, ids.shape, 1)
    for k in range(1, n_mp):
        landing = row_sides.at[lax.rem(mp + n_mp - k, n_mp)]
        remote(landing, landing, gather_send.at[k - 1], gather_recv.at[k - 1], partner).wait_recv()
    sum_side(0)
    by_row = row_sides[...].reshape(pack, 2 * rank)
    chosen = jnp.where(
        which_of(ids) == 0,
        precise(pick, side_sum[0], NT),
        precise(pick, by_row[:, rank:], NT),
    )
    masked[...] = jnp.where((token >= start) & (token < end), chosen, 0.0)
    plain = (((1,), (0,)), ((), ()))
    sketches[0] = precise(masked[...], by_row[:, :rank], plain)

    gate_side = jnp.zeros((pack, rank), F32)
    up_side = jnp.zeros((pack, rank), F32)
    for j in range(n_chunks):
        at = slice(j * chunk, (j + 1) * chunk)
        for g in range(2):
            total = own_part[g, j]
            for k in range(1, n_dp):
                part_copy(g, j, k).wait_recv()
                total = total + recv_part[g, j, k - 1].astype(F32)
            tokens = pl.ds(pl.multiple_of(half_of(g) * half_pack, 16), half_pack)
            gate_grad[tokens, at] = (total * gate_factor[j, tokens, :]).astype(BF16)
            up_grad[tokens, at] = (total * up_factor[j, tokens, :]).astype(BF16)
        gate_side = gate_side + dot_nt(gate_grad[:, at], proj_gate[:, at])
        up_side = up_side + dot_nt(up_grad[:, at], proj_up[:, at])
    send_side(1, gate_side)
    send_side(2, up_side)
    for w in (1, 2):
        sum_side(w)

        @pl.when(needs(mp, w))
        def _():
            product = precise(masked[...], side_sum[w], plain)
            sketches[0] = jnp.where(which_of(row_ids(rank)) == w, product, sketches[0])

    for w in range(3):
        for k in range(1, n_mp):
            @pl.when(needs(lax.rem(mp + k, n_mp), w))
            def _():
                side_copy(w, k).wait_send()
    for copy in sends:
        copy.wait_send()
    for g in range(2):
        for j in range(n_chunks):
            for k in range(1, n_dp):
                part_copy(g, j, k).wait_send()


def flush(*refs):
    for src, dst in zip(refs[:3], refs[3:]):
        dst[...] = src[...]


def local(
    hidden_in,
    out_grad,
    gate_pre,
    up_pre,
    down_weight,
    proj_in,
    proj_grad,
    proj_hidden,
    proj_gate,
    proj_up,
    doc_lengths,
):
    n_dp, n_mp = lax.axis_size("dp"), lax.axis_size("mp")
    own_rows, rank = hidden_in.shape[0], proj_in.shape[0]
    pack, units = gate_pre.shape
    features = down_weight.shape[1]
    docs = doc_lengths.shape[1]
    chunk = 4 * LANES
    if units % chunk:
        chunk = units
    n_chunks = units // chunk
    row_count = 3 * docs * rank // n_mp
    dma = pltpu.SemaphoreType.DMA
    vmem = pl.BlockSpec(memory_space=pltpu.VMEM)
    far = pl.BlockSpec(memory_space=pl.ANY)
    shapes = (
        jax.ShapeDtypeStruct((pack, units), BF16),
        jax.ShapeDtypeStruct((pack, units), BF16),
        jax.ShapeDtypeStruct((1, row_count, rank), F32),
    )
    results = pl.pallas_call(
        functools.partial(kernel, n_dp, n_mp, chunk),
        out_shape=shapes,
        in_specs=[vmem, vmem, pl.BlockSpec(memory_space=pltpu.SMEM)] + [far] * 8,
        out_specs=(vmem, vmem, vmem),
        scratch_shapes=[
            pltpu.VMEM((pack, units), BF16),
            pltpu.VMEM((pack, units), BF16),
            pltpu.VMEM((units, features), BF16),
            pltpu.VMEM(proj_in.shape, BF16),
            pltpu.VMEM(proj_grad.shape, BF16),
            pltpu.VMEM((rank, units), BF16),
            pltpu.VMEM((rank, units), BF16),
            pltpu.VMEM((rank, units), BF16),
            pltpu.VMEM((n_mp, n_dp, own_rows, features), BF16),
            pltpu.VMEM((2, n_dp * pack // 2, features), BF16),
            pltpu.VMEM((2, n_chunks, pack // 2, chunk), F32),
            pltpu.VMEM((2, n_chunks, n_dp - 1, pack // 2, chunk), BF16),
            pltpu.VMEM((2, n_chunks, n_dp - 1, pack // 2, chunk), BF16),
            pltpu.VMEM((n_chunks, pack, chunk), F32),
            pltpu.VMEM((n_chunks, pack, chunk), F32),
            pltpu.VMEM((3, pack // 2, 2 * rank), F32),
            pltpu.VMEM((3, n_mp - 1, pack // 2, 2 * rank), F32),
            pltpu.VMEM((3, pack, rank), F32),
            pltpu.VMEM((n_mp, own_rows, 2 * rank), F32),
            pltpu.VMEM((row_count, pack), F32),
            dma((7,)),
            dma((n_chunks,)),
            dma,
            dma((n_dp - 1,)),
            dma((n_dp - 1,)),
            dma((n_mp // 2 - 1,)),
            dma((n_mp // 2 - 1,)),
            dma((n_mp // 2,)),
            dma((n_mp // 2,)),
            dma((2, n_chunks, n_dp - 1)),
            dma((2, n_chunks, n_dp - 1)),
            dma((3, n_mp - 1)),
            dma((3, n_mp - 1)),
            dma((n_mp - 1,)),
            dma((n_mp - 1,)),
        ],
        compiler_params=pltpu.CompilerParams(
            collective_id=0, has_side_effects=True, vmem_limit_bytes=60 * 1024 * 1024
        ),
    )(
        hidden_in,
        out_grad,
        doc_lengths,
        gate_pre,
        up_pre,
        down_weight,
        proj_in,
        proj_grad,
        proj_hidden,
        proj_gate,
        proj_up,
    )
    return pl.pallas_call(
        flush, out_shape=shapes, in_specs=[vmem] * 3, out_specs=(vmem,) * 3
    )(*results)


def solution(mesh):
    placed = (
        P(("dp", "mp"), None),
        P(("dp", "mp"), None),
        P("dp", "mp"),
        P("dp", "mp"),
        P("mp", "dp"),
        P(),
        P(),
        P(None, "mp"),
        P(None, "mp"),
        P(None, "mp"),
        P("dp", None),
    )
    return jax.shard_map(
        local,
        mesh=mesh,
        in_specs=placed,
        out_specs=(P("dp", "mp"), P("dp", "mp"), P("dp", "mp", None)),
        check_vma=False,
    )
```

```python
import functools

import jax
import jax.numpy as jnp
from jax import lax
from jax.experimental import pallas as pl
from jax.experimental.pallas import tpu as pltpu
from jax.sharding import PartitionSpec as P

LANES = 128
F32 = jnp.float32
BF16 = jnp.bfloat16
NT = (((1,), (1,)), ((), ()))


def dot_nt(a, b):
    return lax.dot_general(a, b, NT, preferred_element_type=F32)


def kernel(
    n_dp,
    n_mp,
    chunk,
    hidden_in,
    out_grad,
    doc_sizes,
    gate_hbm,
    up_hbm,
    weight_hbm,
    proj_in_hbm,
    proj_grad_hbm,
    proj_hidden_hbm,
    proj_gate_hbm,
    proj_up_hbm,
    gate_grad,
    up_grad,
    sketches,
    gate_pre,
    up_pre,
    weight,
    proj_in,
    proj_grad,
    proj_hidden,
    proj_gate,
    proj_up,
    stage,
    lhs,
    own_part,
    send_part,
    recv_part,
    gate_factor,
    up_factor,
    side_part,
    side_in,
    side_sum,
    row_sides,
    masked,
    load_sem,
    weight_sem,
    own_sem,
    turn_send,
    turn_recv,
    row_send,
    row_recv,
    pair_send,
    pair_recv,
    part_send,
    part_recv,
    side_send,
    side_recv,
    gather_send,
    gather_recv,
):
    dp, mp = lax.axis_index("dp"), lax.axis_index("mp")
    pack, units = gate_pre.shape
    own_rows, features = out_grad.shape[0], weight.shape[1]
    rank = proj_in.shape[0]
    n_chunks = units // chunk
    n_row = n_mp // 2
    row, core = mp // 2, mp % 2
    half = n_row // 2
    half_pack = pack // 2
    row_count, docs = sketches.shape[1], doc_sizes.shape[1]
    rank_bits, doc_bits = rank.bit_length() - 1, docs.bit_length() - 1
    mesh_id = pl.DeviceIdType.MESH

    def remote(src, dst, send, recv, device):
        return pltpu.make_async_remote_copy(
            src_ref=src, dst_ref=dst, send_sem=send, recv_sem=recv,
            device_id=device, device_id_type=mesh_id,
        )

    def dp_peer(k):
        return lax.rem(dp + k, n_dp)

    def dp_source(k):
        return lax.rem(dp + n_dp - k, n_dp)

    def half_of(g):
        return row // half if g == 0 else 1 - row // half

    def row_peer(k):
        return half_of(k // half) * half + lax.rem(row % half + k % half, half)

    def row_source(k):
        return half_of(k // half) * half + lax.rem(row % half + half - k % half, half)

    def needs(device, w):
        block = docs * rank
        return (device * row_count < (w + 1) * block) & ((device + 1) * row_count > w * block)

    barrier = pltpu.get_barrier_semaphore()
    for k in range(1, n_dp):
        pl.semaphore_signal(barrier, inc=1, device_id=(dp_peer(k), mp), device_id_type=mesh_id)
    for k in range(1, n_mp):
        pl.semaphore_signal(
            barrier, inc=1, device_id=(dp, lax.rem(mp + k, n_mp)), device_id_type=mesh_id
        )

    own_columns = pl.ds(pl.multiple_of(dp * features, LANES), features)
    own_copy = pltpu.make_async_copy(out_grad.at[:, own_columns], stage.at[mp, dp], own_sem)
    own_copy.start()
    loads = [
        pltpu.make_async_copy(src, dst, load_sem.at[n])
        for n, (src, dst) in enumerate(
            [
                (gate_hbm, gate_pre),
                (up_hbm, up_pre),
                (proj_hidden_hbm, proj_hidden),
                (proj_grad_hbm, proj_grad),
                (proj_in_hbm, proj_in),
                (proj_gate_hbm, proj_gate),
                (proj_up_hbm, proj_up),
            ]
        )
    ]
    for load in loads:
        load.start()

    def weight_load(j):
        rows = pl.ds(pl.multiple_of(j * chunk, 16), chunk)
        return pltpu.make_async_copy(weight_hbm.at[rows], weight.at[rows], weight_sem.at[j])

    for j in range(n_chunks):
        weight_load(j).start()

    pl.semaphore_wait(barrier, n_dp - 1 + n_mp - 1)

    turns = []
    for k in range(1, n_dp):
        peer = dp_peer(k)
        columns = pl.ds(pl.multiple_of(peer * features, LANES), features)
        turn = remote(
            out_grad.at[:, columns], stage.at[mp, dp], turn_send.at[k - 1], turn_recv.at[k - 1],
            (peer, mp),
        )
        turn.start()
        turns.append(turn)
    own_copy.wait()
    for k in range(1, n_dp):
        landing = stage.at[mp, dp_source(k)]
        remote(landing, landing, turn_send.at[k - 1], turn_recv.at[k - 1], (dp, mp)).wait_recv()

    partner = (dp, row * 2 + (1 - core))
    sends = list(turns)
    mine = stage.at[mp]
    copy = remote(mine, mine, pair_send.at[0], pair_recv.at[0], partner)
    copy.start()
    sends.append(copy)
    for k in range(1, n_row):
        copy = remote(
            mine, mine, row_send.at[k - 1], row_recv.at[k - 1], (dp, row_peer(k) * 2 + core)
        )
        copy.start()
        sends.append(copy)

    loads[0].wait()
    loads[1].wait()
    loads[2].wait()
    hidden_side = jnp.zeros((pack, rank), F32)
    for j in range(n_chunks):
        at = slice(j * chunk, (j + 1) * chunk)
        gate_value = gate_pre[:, at].astype(F32)
        up_value = up_pre[:, at].astype(F32)
        sigmoid_gate = 1.0 / (1.0 + jnp.exp(-gate_value))
        silu_gate = gate_value * sigmoid_gate
        hidden = (silu_gate * up_value).astype(BF16)
        gate_factor[j] = up_value * sigmoid_gate * (1.0 + gate_value * (1.0 - sigmoid_gate))
        up_factor[j] = silu_gate
        hidden_side = hidden_side + dot_nt(hidden, proj_hidden[:, at])

    def side_copy(w, k):
        peer = lax.rem(mp + k, n_mp)
        return remote(
            side_part.at[w], side_in.at[w, k - 1], side_send.at[w, k - 1],
            side_recv.at[w, k - 1], (dp, peer),
        )

    def send_side(w, value):
        side_part[w, :, :rank] = value[:half_pack]
        side_part[w, :, rank:] = value[half_pack:]
        for k in range(1, n_mp):
            @pl.when(needs(lax.rem(mp + k, n_mp), w))
            def _():
                side_copy(w, k).start()

    def sum_side(w):
        @pl.when(needs(mp, w))
        def _():
            value = side_part[w]
            for k in range(1, n_mp):
                side_copy(w, k).wait_recv()
                value = value + side_in[w, k - 1]
            side_sum[w, :half_pack] = value[:, :rank]
            side_sum[w, half_pack:] = value[:, rank:]

    side_sum[...] = jnp.zeros(side_sum.shape, F32)
    send_side(0, hidden_side)

    def assemble(g, source_row):
        for k in range(n_dp):
            owner = dp_peer(k)
            both = [stage[source_row * 2 + c, owner].astype(F32) for c in range(2)]
            at = pl.ds(
                pl.multiple_of(k * half_pack + (source_row % half) * 2 * own_rows, 16),
                2 * own_rows,
            )
            lhs[g, at, :] = jnp.concatenate(both, axis=0).astype(BF16)

    def part_copy(g, j, k):
        return remote(
            send_part.at[g, j, k - 1], recv_part.at[g, j, k - 1], part_send.at[g, j, k - 1],
            part_recv.at[g, j, k - 1], (dp_peer(k), mp),
        )

    def half_step(g):
        for k in range(g * half, (g + 1) * half):
            if k == 0:
                continue
            landing = stage.at[row_source(k) * 2 + core]
            remote(landing, landing, row_send.at[k - 1], row_recv.at[k - 1], partner).wait_recv()
            copy = remote(landing, landing, pair_send.at[k], pair_recv.at[k], partner)
            copy.start()
            sends.append(copy)
        for k in range(g * half, (g + 1) * half):
            landing = stage.at[row_source(k) * 2 + (1 - core)]
            remote(landing, landing, pair_send.at[k], pair_recv.at[k], partner).wait_recv()
            assemble(g, row_source(k))

        def multiply(j, carry):
            if g == 0:
                weight_load(j).wait()
            rows = pl.ds(pl.multiple_of(j * chunk, 16), chunk)
            part = dot_nt(lhs[g], weight[rows, :])
            for k in range(1, n_dp):
                send_part[g, j, k - 1] = part[k * half_pack : (k + 1) * half_pack].astype(BF16)
                part_copy(g, j, k).start()
            own_part[g, j] = part[:half_pack]
            return carry

        lax.fori_loop(0, n_chunks, multiply, 0)

    half_step(0)
    half_step(1)
    loads[3].wait()
    row_sides[mp, :, :rank] = dot_nt(out_grad[...], proj_grad[...])
    loads[4].wait()
    row_sides[mp, :, rank:] = dot_nt(hidden_in[...], proj_in[...])
    for k in range(1, n_mp):
        mine = row_sides.at[mp]
        copy = remote(
            mine, mine, gather_send.at[k - 1], gather_recv.at[k - 1], (dp, lax.rem(mp + k, n_mp))
        )
        copy.start()
        sends.append(copy)
    loads[5].wait()
    loads[6].wait()

    def row_ids(columns):
        return mp * row_count + lax.broadcasted_iota(jnp.int32, (row_count, columns), 0)

    def which_of(ids):
        return lax.shift_right_logical(ids, rank_bits + doc_bits)

    def precise(a, b, dims):
        return lax.dot_general(
            a, b, dims, precision=lax.Precision.HIGHEST, preferred_element_type=F32
        )

    ids = row_ids(rank)
    which = which_of(ids)
    column = lax.broadcasted_iota(jnp.int32, ids.shape, 1)
    pick = (column == (ids & (rank - 1))).astype(F32)
    ids = row_ids(pack)
    doc = lax.shift_right_logical(ids, rank_bits) & (docs - 1)
    start = jnp.zeros(ids.shape, jnp.int32)
    end = jnp.zeros(ids.shape, jnp.int32)
    passed = jnp.int32(0)
    for k in range(docs):
        after = passed + doc_sizes[0, k]
        start = jnp.where(doc == k, passed, start)
        end = jnp.where(doc == k, after, end)
        passed = after
    token = lax.broadcasted_iota(jnp.int32, ids.shape, 1)
    for k in range(1, n_mp):
        landing = row_sides.at[lax.rem(mp + n_mp - k, n_mp)]
        remote(landing, landing, gather_send.at[k - 1], gather_recv.at[k - 1], partner).wait_recv()
    sum_side(0)
    by_row = row_sides[...].reshape(pack, 2 * rank)
    chosen = jnp.where(
        which_of(ids) == 0,
        precise(pick, side_sum[0], NT),
        precise(pick, by_row[:, rank:], NT),
    )
    masked[...] = jnp.where((token >= start) & (token < end), chosen, 0.0)
    plain = (((1,), (0,)), ((), ()))
    sketches[0] = precise(masked[...], by_row[:, :rank], plain)

    gate_side = jnp.zeros((pack, rank), F32)
    up_side = jnp.zeros((pack, rank), F32)
    for j in range(n_chunks):
        at = slice(j * chunk, (j + 1) * chunk)
        for g in range(2):
            total = own_part[g, j]
            for k in range(1, n_dp):
                part_copy(g, j, k).wait_recv()
                total = total + recv_part[g, j, k - 1].astype(F32)
            tokens = pl.ds(pl.multiple_of(half_of(g) * half_pack, 16), half_pack)
            gate_grad[tokens, at] = (total * gate_factor[j, tokens, :]).astype(BF16)
            up_grad[tokens, at] = (total * up_factor[j, tokens, :]).astype(BF16)
        gate_side = gate_side + dot_nt(gate_grad[:, at], proj_gate[:, at])
        up_side = up_side + dot_nt(up_grad[:, at], proj_up[:, at])
    send_side(1, gate_side)
    send_side(2, up_side)
    for w in (1, 2):
        sum_side(w)

        @pl.when(needs(mp, w))
        def _():
            product = precise(masked[...], side_sum[w], plain)
            sketches[0] = jnp.where(which_of(row_ids(rank)) == w, product, sketches[0])

    for w in range(3):
        for k in range(1, n_mp):
            @pl.when(needs(lax.rem(mp + k, n_mp), w))
            def _():
                side_copy(w, k).wait_send()
    for copy in sends:
        copy.wait_send()
    for g in range(2):
        for j in range(n_chunks):
            for k in range(1, n_dp):
                part_copy(g, j, k).wait_send()


def flush(*refs):
    for src, dst in zip(refs[:2], refs[3:5]):
        dst[...] = src[...]
    refs[5][0] = refs[2][0].T


def local(
    hidden_in,
    out_grad,
    gate_pre,
    up_pre,
    down_weight,
    proj_in,
    proj_grad,
    proj_hidden,
    proj_gate,
    proj_up,
    doc_lengths,
):
    n_dp, n_mp = lax.axis_size("dp"), lax.axis_size("mp")
    own_rows, rank = hidden_in.shape[0], proj_in.shape[0]
    pack, units = gate_pre.shape
    features = down_weight.shape[1]
    docs = doc_lengths.shape[1]
    chunk = 4 * LANES
    if units % chunk:
        chunk = units
    n_chunks = units // chunk
    row_count = 3 * docs * rank // n_mp
    dma = pltpu.SemaphoreType.DMA
    vmem = pl.BlockSpec(memory_space=pltpu.VMEM)
    far = pl.BlockSpec(memory_space=pl.ANY)
    shapes = (
        jax.ShapeDtypeStruct((pack, units), BF16),
        jax.ShapeDtypeStruct((pack, units), BF16),
        jax.ShapeDtypeStruct((1, row_count, rank), F32),
    )
    results = pl.pallas_call(
        functools.partial(kernel, n_dp, n_mp, chunk),
        out_shape=shapes,
        in_specs=[vmem, vmem, pl.BlockSpec(memory_space=pltpu.SMEM)] + [far] * 8,
        out_specs=(vmem, vmem, vmem),
        scratch_shapes=[
            pltpu.VMEM((pack, units), BF16),
            pltpu.VMEM((pack, units), BF16),
            pltpu.VMEM((units, features), BF16),
            pltpu.VMEM(proj_in.shape, BF16),
            pltpu.VMEM(proj_grad.shape, BF16),
            pltpu.VMEM((rank, units), BF16),
            pltpu.VMEM((rank, units), BF16),
            pltpu.VMEM((rank, units), BF16),
            pltpu.VMEM((n_mp, n_dp, own_rows, features), BF16),
            pltpu.VMEM((2, n_dp * pack // 2, features), BF16),
            pltpu.VMEM((2, n_chunks, pack // 2, chunk), F32),
            pltpu.VMEM((2, n_chunks, n_dp - 1, pack // 2, chunk), BF16),
            pltpu.VMEM((2, n_chunks, n_dp - 1, pack // 2, chunk), BF16),
            pltpu.VMEM((n_chunks, pack, chunk), F32),
            pltpu.VMEM((n_chunks, pack, chunk), F32),
            pltpu.VMEM((3, pack // 2, 2 * rank), F32),
            pltpu.VMEM((3, n_mp - 1, pack // 2, 2 * rank), F32),
            pltpu.VMEM((3, pack, rank), F32),
            pltpu.VMEM((n_mp, own_rows, 2 * rank), F32),
            pltpu.VMEM((row_count, pack), F32),
            dma((7,)),
            dma((n_chunks,)),
            dma,
            dma((n_dp - 1,)),
            dma((n_dp - 1,)),
            dma((n_mp // 2 - 1,)),
            dma((n_mp // 2 - 1,)),
            dma((n_mp // 2,)),
            dma((n_mp // 2,)),
            dma((2, n_chunks, n_dp - 1)),
            dma((2, n_chunks, n_dp - 1)),
            dma((3, n_mp - 1)),
            dma((3, n_mp - 1)),
            dma((n_mp - 1,)),
            dma((n_mp - 1,)),
        ],
        compiler_params=pltpu.CompilerParams(
            collective_id=0, has_side_effects=True, vmem_limit_bytes=60 * 1024 * 1024
        ),
    )(
        hidden_in,
        out_grad,
        doc_lengths,
        gate_pre,
        up_pre,
        down_weight,
        proj_in,
        proj_grad,
        proj_hidden,
        proj_gate,
        proj_up,
    )
    turned = jax.ShapeDtypeStruct((1, rank, row_count), F32)
    gate_grad, up_grad, sketches = pl.pallas_call(
        flush, out_shape=shapes[:2] + (turned,), in_specs=[vmem] * 3, out_specs=(vmem,) * 3
    )(*results)
    return gate_grad, up_grad, jnp.swapaxes(sketches, 1, 2)


def solution(mesh):
    placed = (
        P(("dp", "mp"), None),
        P(("dp", "mp"), None),
        P("dp", "mp"),
        P("dp", "mp"),
        P("mp", "dp"),
        P(),
        P(),
        P(None, "mp"),
        P(None, "mp"),
        P(None, "mp"),
        P("dp", None),
    )
    return jax.shard_map(
        local,
        mesh=mesh,
        in_specs=placed,
        out_specs=(P("dp", "mp"), P("dp", "mp"), P("dp", "mp", None)),
        check_vma=False,
    )
```
